512 devices in a mesh: half: 2 (over z_hi), row: 8 (over y, core), col: 32 (over x, z_lo).
Axes of the slice: x: 4, y: 4, z: 16 (z_hi: 2, z_lo: 8; z = z_hi * 8 + z_lo), core: 2. Of those that a mesh axis runs over, the one named last changes fastest.
Arguments:
- child_updates: float32 [2, 8192, 8192], P('half', 'row', 'col'), may hold values from -6 to 6
- child_maps: int32 [2, 64], replicated, may hold values from 0 to 95, as said below
- panel_pattern: int32 [96, 6], replicated, may hold values 0 or 1
- pivot_inverse: float32 [768, 768], replicated, may hold values from -1 to 1, as said below
Outputs:
- front_out: float32 [8, 2, 768, 12288], P('row', 'half', None, 'col')
The draws below stay inside these ranges and needn't reach their ends.
Inputs may be any that keep to these rules, and one draw needn't show every extreme that they name: child_maps[c, 2 m] and child_maps[c, 2 m + 1] are two different values of 3 m, 3 m + 1, 3 m + 2, the smaller first. `pivot_inverse`: lower triangular with a positive diagonal.
All inputs are finite; a program needn't handle non-finite values.
Results may differ from the reference program's by a relative error of at most 0.000086.
Values sent between devices are 32-bit elements; how exact they have to be, the bound alone decides.
A program may use at most 64 MiB of HBM per device.

```python
import jax
import jax.numpy as jnp
from jax import lax

BLK = 128
NC = 8192
P_SIZE = 768
NF = 12288
NCB = 64
NFB = 96
PB = 6
N_ROW = 8


def draw_child_maps(key, part):
    pairs = NCB // 2
    excluded = jax.random.randint(key, (2, pairs), 0, 3)
    excluded = excluded.at[:, 0].set(jnp.maximum(excluded[:, 0], 1))
    excluded = excluded.at[:, pairs - 1].set(jnp.minimum(excluded[:, pairs - 1], 1))
    starts = 3 * jnp.arange(pairs, dtype=jnp.int32)[None, :]
    lower_pick = starts + (excluded == 0).astype(jnp.int32)
    upper_pick = starts + 2 - (excluded == 2).astype(jnp.int32)
    return jnp.stack([lower_pick, upper_pick], axis=-1).reshape(2, NCB).astype(jnp.int32)


def draw_pivot_inverse(key, part):
    noise_key = jax.random.fold_in(key, 11)
    gain_key = jax.random.fold_in(key, 12)
    row_pos = jnp.arange(P_SIZE)[:, None]
    col_pos = jnp.arange(P_SIZE)[None, :]
    base_scale = P_SIZE ** (-0.25)
    noise = jax.random.truncated_normal(noise_key, -4.0, 4.0, (P_SIZE, P_SIZE), jnp.float32)
    diag_gain = jax.random.uniform(gain_key, (P_SIZE,), jnp.float32, 0.6, 1.2)
    below = (col_pos < row_pos).astype(jnp.float32)
    spread = jnp.sqrt(0.6 / (row_pos.astype(jnp.float32) + 1.0))
    lower_part = noise * base_scale * spread * below
    diagonal = jnp.where(col_pos == row_pos, diag_gain[None, :] * base_scale, 0.0)
    return (lower_part + diagonal).astype(jnp.float32)


def with_ends(drawn, key, low, largest):
    spot = [jax.random.randint(jax.random.fold_in(key, axis), (), 0, length) for axis, length in enumerate(drawn.shape)]
    main_axis = drawn.shape.index(max(drawn.shape))
    next_to = spot[:main_axis] + [(spot[main_axis] + 1) % drawn.shape[main_axis]] + spot[main_axis + 1:]
    return drawn.at[tuple(spot)].set(low).at[tuple(next_to)].set(largest)


def steps_of(key, dims, split, smallest, high):
    level, own = 1.0, jax.random.fold_in(key, 6)
    for dim, shards_of in split:
        heights = jnp.exp(jax.random.uniform(jax.random.fold_in(own, dim), (shards_of,), jnp.float32, smallest / len(split), high / len(split)))
        level = level * jnp.repeat(heights, dims[dim] // shards_of).reshape([-1 if axis == dim else 1 for axis in range(len(dims))])
    return level


def bell_draw(rng, dims, scale, most, shards=(), held_as=jnp.bfloat16):
    array = scale * jax.random.normal(rng, dims, jnp.float32)
    if shards:
        array = array * steps_of(rng, dims, shards, -0.22, 0.18)
    return jnp.clip(array, -most, most).astype(held_as)


def setup_inputs(seed: int = 0) -> dict:
    streams_of = jax.random.split(jax.random.key(seed), 5)
    return {
        "child_updates": bell_draw(streams_of[0], (2, NC, NC), 1.0, 6.0, ((0, 2), (1, 8), (2, 32)), jnp.float32),
        "child_maps": draw_child_maps(jax.random.fold_in(streams_of[4], 71), 0),
        "panel_pattern": with_ends((jax.random.randint(streams_of[2], (NFB, PB), 0, 4) < 3).astype(jnp.int32), jax.random.fold_in(streams_of[2], 1), 0, 1),
        "pivot_inverse": draw_pivot_inverse(jax.random.fold_in(streams_of[4], 71), 0),
    }


def reference(child_updates, child_maps, panel_pattern, pivot_inverse):
    offsets = jnp.arange(BLK, dtype=jnp.int32)
    assembled = jnp.zeros((NF, NF), jnp.float32)
    for member in range(2):
        positions = (child_maps[member][:, None] * BLK + offsets[None, :]).reshape(NC).astype(jnp.int32)
        assembled = assembled.at[positions[:, None], positions[None, :]].add(child_updates[member])
    pattern_mask = jnp.repeat(jnp.repeat(panel_pattern, BLK, axis=0), BLK, axis=1).astype(jnp.float32)
    factor = jnp.dot(assembled[:, :P_SIZE], pivot_inverse.T, precision=lax.Precision.HIGHEST) * pattern_mask
    update = jnp.dot(factor[P_SIZE:], factor[P_SIZE:].T, precision=lax.Precision.HIGHEST)
    trailing = assembled[P_SIZE:, P_SIZE:] - update
    result = assembled.at[:, :P_SIZE].set(factor).at[P_SIZE:, P_SIZE:].set(trailing)
    return result.reshape(N_ROW, 2, NF // (2 * N_ROW), NF)
```

```python
import jax
import jax.numpy as jnp
from jax import lax
from jax.experimental import pallas as pl
from jax.experimental.pallas import tpu as pltpu
from jax.sharding import PartitionSpec as P

BLK = 128
P_SIZE = 768
NF = 12288
MESH = pl.DeviceIdType.MESH


def move_kernel(child, slab_out, col_out, other_out, slab, col, cross, relay, other,
                slab_rx, col_rx, cross_rx, relay_rx, other_rx, tx, loc):
    half = lax.axis_index("half")
    row = lax.axis_index("row")
    colix = lax.axis_index("col")
    y, core = row // 2, row % 2
    x, z = colix // 8, colix % 8
    zz = half * 8 + z

    def at_x(step):
        return (half, row, ((x + step) % 4) * 8 + z)

    def at_z(step):
        return (half, row, x * 8 + (z + step + 8) % 8)

    def at_ring(step):
        there = (zz + step + 16) % 16
        return (there // 8, row, x * 8 + there % 8)

    def at_y(step):
        return (half, ((y + step) % 4) * 2 + core, colix)

    flip = (1 - half, row, colix)
    partner = (half, y * 2 + 1 - core, colix)

    barrier = pltpu.get_barrier_semaphore()
    peers = [at_x(1), at_x(2), at_x(3), at_z(1), at_z(-1), flip, at_ring(4), at_ring(-4),
             at_y(1), at_y(2), at_y(3), partner]
    for peer in peers:
        pl.semaphore_signal(barrier, inc=1, device_id=peer, device_id_type=MESH)
    pl.semaphore_wait(barrier, len(peers))

    pending = []
    count = [0]

    def send(src, dst, rx, device, when=None):
        copy = pltpu.make_async_remote_copy(
            src_ref=src, dst_ref=dst, send_sem=tx.at[count[0]], recv_sem=rx,
            device_id=device, device_id_type=MESH)
        count[0] += 1
        if when is None:
            copy.start()
        else:
            pl.when(when)(copy.start)
        pending.append((copy, when))

    def wait_rx(dst, rx, when=None):
        copy = pltpu.make_async_copy(dst, dst, rx)
        if when is None:
            copy.wait()
        else:
            pl.when(when)(copy.wait)

    def local(src, dst, sem):
        copy = pltpu.make_async_copy(src, dst, sem)
        copy.start()
        return copy

    is_source = (x == 0) & (z < 2)
    is_entry = z < 2
    mine = half * 512
    theirs = (1 - half) * 512
    jz = jnp.minimum(z, 1)

    for q in (2, 1, 3):
        send(child.at[pl.ds(theirs + q * 128, 128)], cross, cross_rx, at_x(q), is_source)
        send(child.at[pl.ds(mine + q * 128, 128)], slab.at[half, jz, q], slab_rx.at[half, jz, q], at_x(q), is_source)

    @pl.when(is_source)
    def _():
        first = local(child.at[pl.ds(theirs, 128)], cross, loc.at[0])
        second = local(child.at[pl.ds(mine, 128)], slab.at[half, jz, 0], loc.at[1])
        first.wait()
        second.wait()

    send(child.at[pl.ds(theirs, 256)], relay.at[0], relay_rx.at[0], at_ring(4))
    send(child.at[pl.ds(theirs + 256, 256)], relay.at[1], relay_rx.at[1], at_ring(-4))

    wait_rx(cross, cross_rx, is_entry & (x > 0))
    send(cross, slab.at[half, jz, x], slab_rx.at[half, jz, x], flip, is_entry)

    def own_piece(k, j, own):
        piece = slab.at[k, j, x]
        rx = slab_rx.at[k, j, x]
        if own:
            wait_rx(piece, rx, (z != j) | (x > 0))
        else:
            wait_rx(piece, rx)
        send(piece, piece, rx, at_z(1), (z >= j) & (z < 7))
        if j == 1:
            send(piece, piece, rx, at_z(-1), z == 1)
        send(piece, piece, rx, at_x(1))
        send(piece, piece, rx, at_x(3))

    for j in (0, 1):
        own_piece(half, j, True)
    for j in (0, 1):
        own_piece(1 - half, j, False)

    for leg, step in ((0, 4), (1, -4)):
        wait_rx(relay.at[leg], relay_rx.at[leg])
        send(relay.at[leg], other.at[leg], other_rx.at[leg], at_ring(step))

    left, right, far = (x + 3) % 4, (x + 1) % 4, (x + 2) % 4
    order = [(half, 0), (half, 1), (1 - half, 0), (1 - half, 1)]
    for k, j in order:
        wait_rx(slab.at[k, j, left], slab_rx.at[k, j, left])
        if j == 0:
            send(slab.at[k, j, left], slab.at[k, j, left], slab_rx.at[k, j, left], at_x(1))
        wait_rx(slab.at[k, j, right], slab_rx.at[k, j, right])
        if j == 1:
            send(slab.at[k, j, right], slab.at[k, j, right], slab_rx.at[k, j, right], at_x(3))
    for k, j in order:
        wait_rx(slab.at[k, j, far], slab_rx.at[k, j, far])

    holder = half == (z // 2) % 2
    lane = core == z // 4
    owner = holder & lane & (y == x)

    @pl.when(owner)
    def _():
        copies = [local(slab.at[m // 2, m % 2, pl.ds(2 * (z % 2), 2)], col.at[m], loc.at[m]) for m in range(4)]
        for copy in copies:
            copy.wait()

    for step in (2, 1, 3):
        to = (y + step) % 4
        send(col.at[to], col.at[to], col_rx.at[to], at_y(step), owner)
    wait_rx(col.at[y], col_rx.at[y], lane & jnp.logical_not(owner))
    send(col.at[y], col.at[y], col_rx.at[y], flip, holder & lane)
    for step in (2, 1, 3):
        to = (y + step) % 4
        send(col.at[y], col.at[y], col_rx.at[y], at_y(step), lane & jnp.logical_not(holder & (to == x)))
    send(col.at[y], col.at[y], col_rx.at[y], partner, lane)
    for step in (1, 3, 2):
        m = (y + step) % 4
        wait_rx(col.at[m], col_rx.at[m], lane & jnp.logical_not(owner))
        send(col.at[m], col.at[m], col_rx.at[m], partner, lane)
    for m in range(4):
        wait_rx(col.at[m], col_rx.at[m], jnp.logical_not(lane))

    outs = [local(slab, slab_out, loc.at[0]), local(col, col_out, loc.at[1])]
    for leg in (0, 1):
        wait_rx(other.at[leg], other_rx.at[leg])
    outs.append(local(other, other_out, loc.at[2]))
    for copy in outs:
        copy.wait()
    for copy, when in pending:
        if when is None:
            copy.wait_send()
        else:
            pl.when(when)(copy.wait_send)


def move(child_tile):
    f32 = jnp.float32
    any_spec = pl.BlockSpec(memory_space=pl.ANY)
    return pl.pallas_call(
        move_kernel,
        out_shape=(jax.ShapeDtypeStruct((2, 2, 4, 128, 256), f32),
                   jax.ShapeDtypeStruct((4, 2, 128, 256), f32),
                   jax.ShapeDtypeStruct((2, 256, 256), f32)),
        in_specs=[any_spec],
        out_specs=(any_spec, any_spec, any_spec),
        scratch_shapes=[
            pltpu.VMEM((2, 2, 4, 128, 256), f32),
            pltpu.VMEM((4, 2, 128, 256), f32),
            pltpu.VMEM((128, 256), f32),
            pltpu.VMEM((2, 256, 256), f32),
            pltpu.VMEM((2, 256, 256), f32),
            pltpu.SemaphoreType.DMA((2, 2, 4)),
            pltpu.SemaphoreType.DMA((4,)),
            pltpu.SemaphoreType.DMA,
            pltpu.SemaphoreType.DMA((2,)),
            pltpu.SemaphoreType.DMA((2,)),
            pltpu.SemaphoreType.DMA((48,)),
            pltpu.SemaphoreType.DMA((4,)),
        ],
        compiler_params=pltpu.CompilerParams(collective_id=0, has_side_effects=True),
    )(child_tile)


def expand_rows(tile, places):
    triples = tile.shape[0] // (2 * BLK)
    pairs = tile.reshape(triples, 2, BLK, tile.shape[1])
    first, second = pairs[:, 0], pairs[:, 1]
    where_first = places[0::2][:, None, None]
    where_second = places[1::2][:, None, None]
    zero = jnp.zeros((), tile.dtype)
    top = jnp.where(where_first == 0, first, zero)
    middle = jnp.where(where_first == 1, first, jnp.where(where_second == 1, second, zero))
    bottom = jnp.where(where_second == 2, second, zero)
    return jnp.stack([top, middle, bottom], axis=1).reshape(triples * 3 * BLK, tile.shape[1])


def expand_cols(tile, places):
    first, second = tile[:, :BLK], tile[:, BLK:]
    zero = jnp.zeros((), tile.dtype)
    return jnp.concatenate([
        jnp.where(places[0] == 0, first, zero),
        jnp.where(places[0] == 1, first, jnp.where(places[1] == 1, second, zero)),
        jnp.where(places[1] == 2, second, zero),
    ], axis=1)


def local(child_updates, child_maps, panel_pattern, pivot_inverse):
    child_tile = child_updates[0]
    half_index = lax.axis_index("half")
    row_index = lax.axis_index("row")
    col_index = lax.axis_index("col")
    slab, col, other = move(child_tile)
    slab_index = 2 * row_index + half_index
    places = child_maps - 3 * (jnp.arange(64, dtype=jnp.int32) // 2)[None, :]
    slab_places = lax.dynamic_slice(places, (0, 4 * slab_index), (2, 4))
    col_places = lax.dynamic_slice(places, (0, 2 * col_index), (2, 2))

    own_rows = lax.dynamic_slice_in_dim(child_tile, half_index * 512, 512, 0)
    other_rows = other.reshape(512, 256)
    first_rows = jnp.where(half_index == 0, own_rows, other_rows)
    second_rows = jnp.where(half_index == 0, other_rows, own_rows)
    assembled = sum(
        expand_cols(expand_rows(t, slab_places[k]), col_places[k])
        for k, t in ((0, first_rows), (1, second_rows)))

    def panel(raw, row_places):
        return jnp.concatenate([
            sum(expand_cols(expand_rows(raw[k][j], row_places[k]), places[k, 2 * j:2 * j + 2]) for k in (0, 1))
            for j in (0, 1)], axis=1)

    slab_panel = panel([[slab[k, j].reshape(512, 256) for j in (0, 1)] for k in (0, 1)], slab_places)
    col_panel = panel([[col[2 * k + j].reshape(256, 256) for j in (0, 1)] for k in (0, 1)], col_places)

    def factor_of(rows, block0, blocks):
        pattern = lax.dynamic_slice_in_dim(panel_pattern, block0, blocks, 0)
        mask = jnp.repeat(jnp.repeat(pattern, BLK, axis=0), BLK, axis=1).astype(jnp.float32)
        return lax.dot_general(rows, pivot_inverse, (((1,), (1,)), ((), ())), precision=lax.Precision.HIGH) * mask

    factor = factor_of(slab_panel, slab_index * 6, 6)
    col_factor = factor_of(col_panel, col_index * 3, 3)
    schur = lax.dot_general(factor, col_factor, (((1,), (1,)), ((), ())), precision=lax.Precision.HIGH)
    pivots = jnp.where(col_index == 0, factor[:, :384], factor[:, 384:])
    result = jnp.where(col_index < 2, pivots, jnp.where(slab_index == 0, assembled, assembled - schur))
    return result.reshape(1, 1, 768, 384)


def solution(mesh):
    placed = (P("half", "row", "col"), P(), P(), P())
    return jax.shard_map(
        local, mesh=mesh, in_specs=placed, out_specs=P("row", "half", None, "col"), check_vma=False
    )
```

```python
import jax
import jax.numpy as jnp
from jax import lax
from jax.experimental import pallas as pl
from jax.experimental.pallas import tpu as pltpu
from jax.sharding import PartitionSpec as P

BLK = 128
P_SIZE = 768
NF = 12288
MESH = pl.DeviceIdType.MESH


def move_kernel(child, slab_out, col_out, other_out, slab, col, cross, relay, other,
                slab_rx, col_rx, cross_rx, relay_rx, other_rx, tx, loc):
    half = lax.axis_index("half")
    row = lax.axis_index("row")
    colix = lax.axis_index("col")
    y, core = row // 2, row % 2
    x, z = colix // 8, colix % 8
    zz = half * 8 + z

    def at_x(step):
        return (half, row, ((x + step) % 4) * 8 + z)

    def at_z(step):
        return (half, row, x * 8 + (z + step + 8) % 8)

    def at_ring(step):
        there = (zz + step + 16) % 16
        return (there // 8, row, x * 8 + there % 8)

    def at_y(step):
        return (half, ((y + step) % 4) * 2 + core, colix)

    flip = (1 - half, row, colix)
    partner = (half, y * 2 + 1 - core, colix)

    barrier = pltpu.get_barrier_semaphore()
    peers = [at_x(1), at_x(2), at_x(3), at_z(1), at_z(-1), flip, at_ring(4), at_ring(-4),
             at_y(1), at_y(2), at_y(3), partner]
    for peer in peers:
        pl.semaphore_signal(barrier, inc=1, device_id=peer, device_id_type=MESH)
    pl.semaphore_wait(barrier, len(peers))

    pending = []
    count = [0]

    def send(src, dst, rx, device, when=None):
        copy = pltpu.make_async_remote_copy(
            src_ref=src, dst_ref=dst, send_sem=tx.at[count[0]], recv_sem=rx,
            device_id=device, device_id_type=MESH)
        count[0] += 1
        if when is None:
            copy.start()
        else:
            pl.when(when)(copy.start)
        pending.append((copy, when))

    def wait_rx(dst, rx, when=None):
        copy = pltpu.make_async_copy(dst, dst, rx)
        if when is None:
            copy.wait()
        else:
            pl.when(when)(copy.wait)

    def local(src, dst, sem):
        copy = pltpu.make_async_copy(src, dst, sem)
        copy.start()
        return copy

    is_source = (x == 0) & (z < 2)
    is_entry = z < 2
    mine = half * 512
    theirs = (1 - half) * 512
    jz = jnp.minimum(z, 1)

    for q in (2, 1, 3):
        send(child.at[pl.ds(theirs + q * 128, 128)], cross, cross_rx, at_x(q), is_source)
        send(child.at[pl.ds(mine + q * 128, 128)], slab.at[half, jz, q], slab_rx.at[half, jz, q], at_x(q), is_source)

    @pl.when(is_source)
    def _():
        first = local(child.at[pl.ds(theirs, 128)], cross, loc.at[0])
        second = local(child.at[pl.ds(mine, 128)], slab.at[half, jz, 0], loc.at[1])
        first.wait()
        second.wait()

    send(child.at[pl.ds(theirs, 256)], relay.at[0], relay_rx.at[0], at_ring(4))
    send(child.at[pl.ds(theirs + 256, 256)], relay.at[1], relay_rx.at[1], at_ring(-4))

    wait_rx(cross, cross_rx, is_entry & (x > 0))
    send(cross, slab.at[half, jz, x], slab_rx.at[half, jz, x], flip, is_entry)

    def own_piece(k, j, own):
        piece = slab.at[k, j, x]
        rx = slab_rx.at[k, j, x]
        if own:
            wait_rx(piece, rx, (z != j) | (x > 0))
        else:
            wait_rx(piece, rx)
        send(piece, piece, rx, at_z(1), (z >= j) & (z < 7))
        if j == 1:
            send(piece, piece, rx, at_z(-1), z == 1)
        send(piece, piece, rx, at_x(1))
        send(piece, piece, rx, at_x(3))

    for j in (0, 1):
        own_piece(half, j, True)
    for j in (0, 1):
        own_piece(1 - half, j, False)

    for leg, step in ((0, 4), (1, -4)):
        wait_rx(relay.at[leg], relay_rx.at[leg])
        send(relay.at[leg], other.at[leg], other_rx.at[leg], at_ring(step))

    left, right, far = (x + 3) % 4, (x + 1) % 4, (x + 2) % 4
    order = [(half, 0), (half, 1), (1 - half, 0), (1 - half, 1)]
    for k, j in order:
        wait_rx(slab.at[k, j, left], slab_rx.at[k, j, left])
        if j == 0:
            send(slab.at[k, j, left], slab.at[k, j, left], slab_rx.at[k, j, left], at_x(1))
        wait_rx(slab.at[k, j, right], slab_rx.at[k, j, right])
        if j == 1:
            send(slab.at[k, j, right], slab.at[k, j, right], slab_rx.at[k, j, right], at_x(3))
    for k, j in order:
        wait_rx(slab.at[k, j, far], slab_rx.at[k, j, far])

    holder = half == (z // 2) % 2
    lane = core == z // 4
    owner = holder & lane & (y == x)

    @pl.when(owner)
    def _():
        copies = [local(slab.at[m // 2, m % 2, pl.ds(2 * (z % 2), 2)], col.at[m], loc.at[m]) for m in range(4)]
        for copy in copies:
            copy.wait()

    for step in (2, 1, 3):
        to = (y + step) % 4
        send(col.at[to], col.at[to], col_rx.at[to], at_y(step), owner)
    wait_rx(col.at[y], col_rx.at[y], lane & jnp.logical_not(owner))
    send(col.at[y], col.at[y], col_rx.at[y], flip, holder & lane)
    for step in (2, 1, 3):
        to = (y + step) % 4
        send(col.at[y], col.at[y], col_rx.at[y], at_y(step), lane & jnp.logical_not(holder & (to == x)))
    send(col.at[y], col.at[y], col_rx.at[y], partner, lane)
    for step in (1, 3, 2):
        m = (y + step) % 4
        wait_rx(col.at[m], col_rx.at[m], lane & jnp.logical_not(owner))
        send(col.at[m], col.at[m], col_rx.at[m], partner, lane)
    for m in range(4):
        wait_rx(col.at[m], col_rx.at[m], jnp.logical_not(lane))

    outs = [local(slab, slab_out, loc.at[0]), local(col, col_out, loc.at[1])]
    for leg in (0, 1):
        wait_rx(other.at[leg], other_rx.at[leg])
    outs.append(local(other, other_out, loc.at[2]))
    for copy in outs:
        copy.wait()
    for copy, when in pending:
        if when is None:
            copy.wait_send()
        else:
            pl.when(when)(copy.wait_send)


def move(child_tile):
    f32 = jnp.float32
    any_spec = pl.BlockSpec(memory_space=pl.ANY)
    return pl.pallas_call(
        move_kernel,
        out_shape=(jax.ShapeDtypeStruct((2, 2, 4, 128, 256), f32),
                   jax.ShapeDtypeStruct((4, 2, 128, 256), f32),
                   jax.ShapeDtypeStruct((2, 256, 256), f32)),
        in_specs=[any_spec],
        out_specs=(any_spec, any_spec, any_spec),
        scratch_shapes=[
            pltpu.VMEM((2, 2, 4, 128, 256), f32),
            pltpu.VMEM((4, 2, 128, 256), f32),
            pltpu.VMEM((128, 256), f32),
            pltpu.VMEM((2, 256, 256), f32),
            pltpu.VMEM((2, 256, 256), f32),
            pltpu.SemaphoreType.DMA((2, 2, 4)),
            pltpu.SemaphoreType.DMA((4,)),
            pltpu.SemaphoreType.DMA,
            pltpu.SemaphoreType.DMA((2,)),
            pltpu.SemaphoreType.DMA((2,)),
            pltpu.SemaphoreType.DMA((48,)),
            pltpu.SemaphoreType.DMA((4,)),
        ],
        compiler_params=pltpu.CompilerParams(collective_id=0, has_side_effects=True),
    )(child_tile)


def split(value):
    high = value.astype(jnp.bfloat16)
    return high, (value - high.astype(jnp.float32)).astype(jnp.bfloat16)


def dot3(a_high, a_low, b_high, b_low):
    def dot(a, b):
        return lax.dot_general(a, b, (((1,), (1,)), ((), ())), preferred_element_type=jnp.float32)
    return dot(a_high, b_high) + (dot(a_high, b_low) + dot(a_low, b_high))


def weights(maps, k, triple):
    first = maps[k, 2 * triple] - 3 * triple
    second = maps[k, 2 * triple + 1] - 3 * triple
    return [jnp.where(t, 1.0, 0.0).astype(jnp.float32) for t in (first == 0, first == 1, second == 1, second == 2)]


def expand(pairs, row_weights, col_weights):
    total = [[None] * 3 for _ in range(3)]
    for (first, second), rw, cw in zip(pairs, row_weights, col_weights):
        rows = (first * rw[0], first * rw[1] + second * rw[2], second * rw[3])
        for p, value in enumerate(rows):
            left, right = value[:, :BLK], value[:, BLK:]
            for q, part in enumerate((left * cw[0], left * cw[1] + right * cw[2], right * cw[3])):
                total[p][q] = part if total[p][q] is None else total[p][q] + part
    return total


def front_kernel(maps, pattern, inverse, child, other, slab, col, out,
                 inv_high, inv_low, tile_high, tile_low, fac_high, fac_low):
    half = lax.axis_index("half")
    row = lax.axis_index("row")
    colix = lax.axis_index("col")
    slab_index = 2 * row + half
    for b in range(6):
        rows = slice(b * BLK, (b + 1) * BLK)
        inv_high[rows], inv_low[rows] = split(inverse[rows])
    panel_cols = [[weights(maps, k, j) for k in (0, 1)] for j in (0, 1)]
    for t in range(3):
        triple = 2 * slab_index + t if t < 2 else colix
        row_weights = [weights(maps, k, triple) for k in (0, 1)]
        for j in range(2):
            if t < 2:
                pairs = [(slab[k, j, 2 * t], slab[k, j, 2 * t + 1]) for k in (0, 1)]
            else:
                pairs = [(col[2 * k + j, 0], col[2 * k + j, 1]) for k in (0, 1)]
            blocks = expand(pairs, row_weights, panel_cols[j])
            for p in range(3):
                for q in range(3):
                    high, low = split(blocks[p][q])
                    where = (slice(p * BLK, (p + 1) * BLK), slice((3 * j + q) * BLK, (3 * j + q + 1) * BLK))
                    tile_high[t, where[0], where[1]] = high
                    tile_low[t, where[0], where[1]] = low
        for n in range(3):
            depth = (n + 1) * 256
            cols = slice(n * 256, depth)
            product = dot3(tile_high[t, :, :depth], tile_low[t, :, :depth],
                           inv_high[cols, :depth], inv_low[cols, :depth])
            for p in range(3):
                for q in range(2):
                    b = 2 * n + q
                    block = product[p * BLK:(p + 1) * BLK, q * BLK:(q + 1) * BLK]
                    block = block * pattern[3 * triple + p, b].astype(jnp.float32)
                    rows = slice(t * 384 + p * BLK, t * 384 + (p + 1) * BLK)
                    high, low = split(block)
                    fac_high[rows, b * BLK:(b + 1) * BLK] = high
                    fac_low[rows, b * BLK:(b + 1) * BLK] = low
                    if t < 2:
                        @pl.when(colix == b // 3)
                        def _(rows=rows, b=b, block=block):
                            out[rows, (b % 3) * BLK:(b % 3 + 1) * BLK] = block

    @pl.when(colix >= 2)
    def _():
        col_weights = [weights(maps, k, colix) for k in (0, 1)]
        keep = slab_index == 0
        for t in range(2):
            schur = dot3(fac_high[t * 384:(t + 1) * 384], fac_low[t * 384:(t + 1) * 384],
                         fac_high[768:], fac_low[768:])
            row_weights = [weights(maps, k, 2 * slab_index + t) for k in (0, 1)]
            own = [child[pl.ds(half * 512 + t * 256 + i * BLK, BLK), :] for i in (0, 1)]
            sent = [other[t, i * BLK:(i + 1) * BLK, :] for i in (0, 1)]
            ordered = [[jnp.where(half == k, a, b) for a, b in zip(own, sent)] for k in (0, 1)]
            blocks = expand(ordered, row_weights, col_weights)
            for p in range(3):
                for q in range(3):
                    term = schur[p * BLK:(p + 1) * BLK, q * BLK:(q + 1) * BLK]
                    out[t * 384 + p * BLK:t * 384 + (p + 1) * BLK, q * BLK:(q + 1) * BLK] = (
                        blocks[p][q] - jnp.where(keep, 0.0, term))


def local(child_updates, child_maps, panel_pattern, pivot_inverse):
    child_tile = child_updates[0]
    slab, col, other = move(child_tile)
    smem = pl.BlockSpec(memory_space=pltpu.SMEM)
    vmem = pl.BlockSpec(memory_space=pltpu.VMEM)
    bf16 = jnp.bfloat16
    result = pl.pallas_call(
        front_kernel,
        out_shape=jax.ShapeDtypeStruct((768, 384), jnp.float32),
        in_specs=[smem, smem] + [vmem] * 5,
        out_specs=vmem,
        scratch_shapes=[
            pltpu.VMEM((768, 768), bf16),
            pltpu.VMEM((768, 768), bf16),
            pltpu.VMEM((3, 384, 768), bf16),
            pltpu.VMEM((3, 384, 768), bf16),
            pltpu.VMEM((1152, 768), bf16),
            pltpu.VMEM((1152, 768), bf16),
        ],
        compiler_params=pltpu.CompilerParams(vmem_limit_bytes=48 * 2**20),
    )(child_maps, panel_pattern, pivot_inverse, child_tile, other, slab, col)
    return result.reshape(1, 1, 768, 384)


def solution(mesh):
    placed = (P("half", "row", "col"), P(), P(), P())
    return jax.shard_map(
        local, mesh=mesh, in_specs=placed, out_specs=P("row", "half", None, "col"), check_vma=False
    )
```

```python
import jax
import jax.numpy as jnp
from jax import lax
from jax.experimental import pallas as pl
from jax.experimental.pallas import tpu as pltpu
from jax.sharding import PartitionSpec as P

BLK = 128
P_SIZE = 768
NF = 12288
MESH = pl.DeviceIdType.MESH
PARTS = 2
LAG = 2


def move_kernel(child, slab_out, col_out, other_out, slab, col, cross, other,
                slab_rx, col_rx, cross_rx, other_rx, tx, loc, cross_loc):
    half = lax.axis_index("half")
    row = lax.axis_index("row")
    colix = lax.axis_index("col")
    y, core = row // 2, row % 2
    x, z = colix // 8, colix % 8

    def at_x(step):
        return (half, row, ((x + step) % 4) * 8 + z)

    def at_z(step):
        return (half, row, x * 8 + (z + step + 8) % 8)

    def at_y(step):
        return (half, ((y + step) % 4) * 2 + core, colix)

    flip = (1 - half, row, colix)
    partner = (half, y * 2 + 1 - core, colix)

    barrier = pltpu.get_barrier_semaphore()
    peers = [at_x(1), at_x(2), at_x(3), at_z(1), at_z(-1), flip,
             at_y(1), at_y(2), at_y(3), partner]
    for peer in peers:
        pl.semaphore_signal(barrier, inc=1, device_id=peer, device_id_type=MESH)
    pl.semaphore_wait(barrier, len(peers))

    pending = []
    count = [0]

    def send(src, dst, rx, device, when=None):
        copy = pltpu.make_async_remote_copy(
            src_ref=src, dst_ref=dst, send_sem=tx.at[count[0]], recv_sem=rx,
            device_id=device, device_id_type=MESH)
        count[0] += 1
        if when is None:
            copy.start()
        else:
            pl.when(when)(copy.start)
        pending.append((copy, when))

    def wait_rx(dst, rx, when=None):
        copy = pltpu.make_async_copy(dst, dst, rx)
        if when is None:
            copy.wait()
        else:
            pl.when(when)(copy.wait)

    def local(src, dst, sem):
        copy = pltpu.make_async_copy(src, dst, sem)
        copy.start()
        return copy

    is_source = (x == 0) & (z < 2)
    is_entry = z < 2
    mine = half * 512
    theirs = (1 - half) * 512
    jz = jnp.minimum(z, 1)

    part = BLK // PARTS

    def rows_of(start, s):
        return pl.ds(start + s * part, part)

    for s in range(PARTS):
        for q in (2, 1, 3):
            send(child.at[rows_of(theirs + q * 128, s)], cross.at[s], cross_rx.at[s], at_x(q), is_source)
            send(child.at[rows_of(mine + q * 128, s)], slab.at[half, jz, q, rows_of(0, s)],
                 slab_rx.at[half, jz, q, s], at_x(q), is_source)

    @pl.when(is_source)
    def _():
        copies = [local(child.at[pl.ds(mine, 128)], slab.at[half, jz, 0], loc.at[0])]
        copies += [local(child.at[rows_of(theirs, s)], cross.at[s], cross_loc.at[s]) for s in range(PARTS)]
        for copy in copies:
            copy.wait()

    def exchange(i):
        send(child.at[pl.ds(theirs + 64 * i, 64)], other.at[i], other_rx.at[i], flip)

    exchange(0)
    exchange(1)
    left, right, far = (x + 3) % 4, (x + 1) % 4, (x + 2) % 4

    def piece_of(k, j, q, s):
        return slab.at[k, j, q, rows_of(0, s)], slab_rx.at[k, j, q, s]

    def own_piece(k, j, s, own):
        piece, rx = piece_of(k, j, x, s)
        if own:
            wait_rx(piece, rx, (z != j) | (x > 0))
        else:
            wait_rx(piece, rx)
        send(piece, piece, rx, at_z(1), (z >= j) & (z < 7))
        if j == 1:
            send(piece, piece, rx, at_z(-1), z == 1)
        send(piece, piece, rx, at_x(1))
        send(piece, piece, rx, at_x(3))

    def side_pieces(k, j, s):
        piece, rx = piece_of(k, j, left, s)
        wait_rx(piece, rx)
        if j == 0:
            send(piece, piece, rx, at_x(1))
        piece, rx = piece_of(k, j, right, s)
        wait_rx(piece, rx)
        if j == 1:
            send(piece, piece, rx, at_x(3))

    for s in range(PARTS):
        wait_rx(cross.at[s], cross_rx.at[s], is_entry & (x > 0))
        piece, rx = piece_of(half, jz, x, s)
        send(cross.at[s], piece, rx, flip, is_entry)
    order = [(own, j, s) for own in (True, False) for s in range(PARTS) for j in (0, 1)]
    for at, (own, j, s) in enumerate(order):
        own_piece(half if own else 1 - half, j, s, own)
        if at + 2 < 8:
            exchange(at + 2)
        if at >= LAG:
            own, j, s = order[at - LAG]
            side_pieces(half if own else 1 - half, j, s)
    for own, j, s in order[len(order) - LAG:]:
        side_pieces(half if own else 1 - half, j, s)
    for own, j, s in order:
        piece, rx = piece_of(half if own else 1 - half, j, far, s)
        wait_rx(piece, rx)

    holder = half == (z // 2) % 2
    lane = core == z // 4
    owner = holder & lane & (y == x)

    @pl.when(owner)
    def _():
        copies = [local(slab.at[m // 2, m % 2, pl.ds(2 * (z % 2), 2)], col.at[m], loc.at[m]) for m in range(4)]
        for copy in copies:
            copy.wait()

    for step in (2, 1, 3):
        to = (y + step) % 4
        send(col.at[to], col.at[to], col_rx.at[to], at_y(step), owner)
    wait_rx(col.at[y], col_rx.at[y], lane & jnp.logical_not(owner))
    send(col.at[y], col.at[y], col_rx.at[y], flip, holder & lane)
    for step in (2, 1, 3):
        to = (y + step) % 4
        send(col.at[y], col.at[y], col_rx.at[y], at_y(step), lane & jnp.logical_not(holder & (to == x)))
    send(col.at[y], col.at[y], col_rx.at[y], partner, lane)
    for step in (1, 3, 2):
        m = (y + step) % 4
        wait_rx(col.at[m], col_rx.at[m], lane & jnp.logical_not(owner))
        send(col.at[m], col.at[m], col_rx.at[m], partner, lane)
    for m in range(4):
        wait_rx(col.at[m], col_rx.at[m], jnp.logical_not(lane))

    outs = [local(slab, slab_out, loc.at[0]), local(col, col_out, loc.at[1])]
    for i in range(8):
        wait_rx(other.at[i], other_rx.at[i])
    outs.append(local(other, other_out, loc.at[2]))
    for copy in outs:
        copy.wait()
    for copy, when in pending:
        if when is None:
            copy.wait_send()
        else:
            pl.when(when)(copy.wait_send)


def move(child_tile):
    f32 = jnp.float32
    any_spec = pl.BlockSpec(memory_space=pl.ANY)
    return pl.pallas_call(
        move_kernel,
        out_shape=(jax.ShapeDtypeStruct((2, 2, 4, 128, 256), f32),
                   jax.ShapeDtypeStruct((4, 2, 128, 256), f32),
                   jax.ShapeDtypeStruct((8, 64, 256), f32)),
        in_specs=[any_spec],
        out_specs=(any_spec, any_spec, any_spec),
        scratch_shapes=[
            pltpu.VMEM((2, 2, 4, 128, 256), f32),
            pltpu.VMEM((4, 2, 128, 256), f32),
            pltpu.VMEM((PARTS, 128 // PARTS, 256), f32),
            pltpu.VMEM((8, 64, 256), f32),
            pltpu.SemaphoreType.DMA((2, 2, 4, PARTS)),
            pltpu.SemaphoreType.DMA((4,)),
            pltpu.SemaphoreType.DMA((PARTS,)),
            pltpu.SemaphoreType.DMA((8,)),
            pltpu.SemaphoreType.DMA((32 + 32 * PARTS,)),
            pltpu.SemaphoreType.DMA((4,)),
            pltpu.SemaphoreType.DMA((PARTS,)),
        ],
        compiler_params=pltpu.CompilerParams(collective_id=0, has_side_effects=True),
    )(child_tile)


def split(value):
    high = value.astype(jnp.bfloat16)
    return high, (value - high.astype(jnp.float32)).astype(jnp.bfloat16)


def dot3(a_high, a_low, b_high, b_low):
    def dot(a, b):
        return lax.dot_general(a, b, (((1,), (1,)), ((), ())), preferred_element_type=jnp.float32)
    return dot(a_high, b_high) + (dot(a_high, b_low) + dot(a_low, b_high))


def weights(maps, k, triple):
    first = maps[k, 2 * triple] - 3 * triple
    second = maps[k, 2 * triple + 1] - 3 * triple
    return [jnp.where(t, 1.0, 0.0).astype(jnp.float32) for t in (first == 0, first == 1, second == 1, second == 2)]


def expand(pairs, row_weights, col_weights):
    total = [[None] * 3 for _ in range(3)]
    for (first, second), rw, cw in zip(pairs, row_weights, col_weights):
        rows = (first * rw[0], first * rw[1] + second * rw[2], second * rw[3])
        for p, value in enumerate(rows):
            left, right = value[:, :BLK], value[:, BLK:]
            for q, part in enumerate((left * cw[0], left * cw[1] + right * cw[2], right * cw[3])):
                total[p][q] = part if total[p][q] is None else total[p][q] + part
    return total


def front_kernel(maps, pattern, inverse, child, other, slab, col, out,
                 inv_high, inv_low, tile_high, tile_low, fac_high, fac_low):
    half = lax.axis_index("half")
    row = lax.axis_index("row")
    colix = lax.axis_index("col")
    slab_index = 2 * row + half
    for b in range(6):
        rows = slice(b * BLK, (b + 1) * BLK)
        inv_high[rows], inv_low[rows] = split(inverse[rows])
    panel_cols = [[weights(maps, k, j) for k in (0, 1)] for j in (0, 1)]
    for t in range(3):
        triple = 2 * slab_index + t if t < 2 else colix
        row_weights = [weights(maps, k, triple) for k in (0, 1)]
        for j in range(2):
            if t < 2:
                pairs = [(slab[k, j, 2 * t], slab[k, j, 2 * t + 1]) for k in (0, 1)]
            else:
                pairs = [(col[2 * k + j, 0], col[2 * k + j, 1]) for k in (0, 1)]
            blocks = expand(pairs, row_weights, panel_cols[j])
            for p in range(3):
                for q in range(3):
                    high, low = split(blocks[p][q])
                    where = (slice(p * BLK, (p + 1) * BLK), slice((3 * j + q) * BLK, (3 * j + q + 1) * BLK))
                    tile_high[t, where[0], where[1]] = high
                    tile_low[t, where[0], where[1]] = low
        for n in range(3):
            depth = (n + 1) * 256
            cols = slice(n * 256, depth)
            product = dot3(tile_high[t, :, :depth], tile_low[t, :, :depth],
                           inv_high[cols, :depth], inv_low[cols, :depth])
            for p in range(3):
                for q in range(2):
                    b = 2 * n + q
                    block = product[p * BLK:(p + 1) * BLK, q * BLK:(q + 1) * BLK]
                    block = block * pattern[3 * triple + p, b].astype(jnp.float32)
                    rows = slice(t * 384 + p * BLK, t * 384 + (p + 1) * BLK)
                    high, low = split(block)
                    fac_high[rows, b * BLK:(b + 1) * BLK] = high
                    fac_low[rows, b * BLK:(b + 1) * BLK] = low
                    if t < 2:
                        @pl.when(colix == b // 3)
                        def _(rows=rows, b=b, block=block):
                            out[rows, (b % 3) * BLK:(b % 3 + 1) * BLK] = block

    @pl.when(colix >= 2)
    def _():
        col_weights = [weights(maps, k, colix) for k in (0, 1)]
        keep = slab_index == 0
        for t in range(2):
            schur = dot3(fac_high[t * 384:(t + 1) * 384], fac_low[t * 384:(t + 1) * 384],
                         fac_high[768:], fac_low[768:])
            row_weights = [weights(maps, k, 2 * slab_index + t) for k in (0, 1)]
            own = [child[pl.ds(half * 512 + t * 256 + i * BLK, BLK), :] for i in (0, 1)]
            sent = [other[4 * t + 2 * i:4 * t + 2 * i + 2].reshape(BLK, 256) for i in (0, 1)]
            ordered = [[jnp.where(half == k, a, b) for a, b in zip(own, sent)] for k in (0, 1)]
            blocks = expand(ordered, row_weights, col_weights)
            for p in range(3):
                for q in range(3):
                    term = schur[p * BLK:(p + 1) * BLK, q * BLK:(q + 1) * BLK]
                    out[t * 384 + p * BLK:t * 384 + (p + 1) * BLK, q * BLK:(q + 1) * BLK] = (
                        blocks[p][q] - jnp.where(keep, 0.0, term))


def local(child_updates, child_maps, panel_pattern, pivot_inverse):
    child_tile = child_updates[0]
    slab, col, other = move(child_tile)
    smem = pl.BlockSpec(memory_space=pltpu.SMEM)
    vmem = pl.BlockSpec(memory_space=pltpu.VMEM)
    bf16 = jnp.bfloat16
    result = pl.pallas_call(
        front_kernel,
        out_shape=jax.ShapeDtypeStruct((768, 384), jnp.float32),
        in_specs=[smem, smem] + [vmem] * 5,
        out_specs=vmem,
        scratch_shapes=[
            pltpu.VMEM((768, 768), bf16),
            pltpu.VMEM((768, 768), bf16),
            pltpu.VMEM((3, 384, 768), bf16),
            pltpu.VMEM((3, 384, 768), bf16),
            pltpu.VMEM((1152, 768), bf16),
            pltpu.VMEM((1152, 768), bf16),
        ],
        compiler_params=pltpu.CompilerParams(vmem_limit_bytes=48 * 2**20),
    )(child_maps, panel_pattern, pivot_inverse, child_tile, other, slab, col)
    return result.reshape(1, 1, 768, 384)


def solution(mesh):
    placed = (P("half", "row", "col"), P(), P(), P())
    return jax.shard_map(
        local, mesh=mesh, in_specs=placed, out_specs=P("row", "half", None, "col"), check_vma=False
    )
```

```python
import jax
import jax.numpy as jnp
from jax import lax
from jax.experimental import pallas as pl
from jax.experimental.pallas import tpu as pltpu
from jax.sharding import PartitionSpec as P

BLK = 128
P_SIZE = 768
NF = 12288
MESH = pl.DeviceIdType.MESH
PARTS = 2
LAG = 2


def move_kernel(child, slab_out, col_out, other_out, slab, col, cross, other,
                slab_rx, col_rx, cross_rx, other_rx, tx, loc, cross_loc):
    half = lax.axis_index("half")
    row = lax.axis_index("row")
    colix = lax.axis_index("col")
    y, core = row // 2, row % 2
    x, z = colix // 8, colix % 8

    def at_x(step):
        return (half, row, ((x + step) % 4) * 8 + z)

    def at_z(step):
        return (half, row, x * 8 + (z + step + 8) % 8)

    def at_y(step):
        return (half, ((y + step) % 4) * 2 + core, colix)

    flip = (1 - half, row, colix)
    partner = (half, y * 2 + 1 - core, colix)

    barrier = pltpu.get_barrier_semaphore()
    peers = [at_x(1), at_x(2), at_x(3), at_z(1), at_z(-1), flip,
             at_y(1), at_y(2), at_y(3), partner]
    for peer in peers:
        pl.semaphore_signal(barrier, inc=1, device_id=peer, device_id_type=MESH)
    pl.semaphore_wait(barrier, len(peers))

    pending = []
    count = [0]

    def send(src, dst, rx, device, when=None):
        copy = pltpu.make_async_remote_copy(
            src_ref=src, dst_ref=dst, send_sem=tx.at[count[0]], recv_sem=rx,
            device_id=device, device_id_type=MESH)
        count[0] += 1
        if when is None:
            copy.start()
        else:
            pl.when(when)(copy.start)
        pending.append((copy, when))

    def wait_rx(dst, rx, when=None):
        copy = pltpu.make_async_copy(dst, dst, rx)
        if when is None:
            copy.wait()
        else:
            pl.when(when)(copy.wait)

    def local(src, dst, sem):
        copy = pltpu.make_async_copy(src, dst, sem)
        copy.start()
        return copy

    is_source = (x == 0) & (z < 2)
    is_entry = z < 2
    mine = half * 512
    theirs = (1 - half) * 512
    jz = jnp.minimum(z, 1)

    part = BLK // PARTS

    def rows_of(start, s):
        return pl.ds(start + s * part, part)

    for s in range(PARTS):
        for q in (2, 1, 3):
            send(child.at[rows_of(theirs + q * 128, s)], cross.at[s], cross_rx.at[s], at_x(q), is_source)
            send(child.at[rows_of(mine + q * 128, s)], slab.at[half, jz, q, rows_of(0, s)],
                 slab_rx.at[half, jz, q, s], at_x(q), is_source)

    @pl.when(is_source)
    def _():
        copies = [local(child.at[pl.ds(mine, 128)], slab.at[half, jz, 0], loc.at[0])]
        copies += [local(child.at[rows_of(theirs, s)], cross.at[s], cross_loc.at[s]) for s in range(PARTS)]
        for copy in copies:
            copy.wait()

    def exchange(i):
        send(child.at[pl.ds(theirs + 64 * i, 64)], other.at[i], other_rx.at[i], flip)

    exchange(0)
    exchange(1)
    left, right, far = (x + 3) % 4, (x + 1) % 4, (x + 2) % 4

    def piece_of(k, j, q, s):
        return slab.at[k, j, q, rows_of(0, s)], slab_rx.at[k, j, q, s]

    def own_piece(k, j, s, own):
        piece, rx = piece_of(k, j, x, s)
        if own:
            wait_rx(piece, rx, (z != j) | (x > 0))
        else:
            wait_rx(piece, rx)
        send(piece, piece, rx, at_z(1), (z >= j) & (z < 7))
        if j == 1:
            send(piece, piece, rx, at_z(-1), z == 1)
        send(piece, piece, rx, at_x(1))
        send(piece, piece, rx, at_x(3))

    def side_pieces(k, j, s):
        piece, rx = piece_of(k, j, left, s)
        wait_rx(piece, rx)
        if j == 0:
            send(piece, piece, rx, at_x(1))
        piece, rx = piece_of(k, j, right, s)
        wait_rx(piece, rx)
        if j == 1:
            send(piece, piece, rx, at_x(3))

    for s in range(PARTS):
        wait_rx(cross.at[s], cross_rx.at[s], is_entry & (x > 0))
        piece, rx = piece_of(half, jz, x, s)
        send(cross.at[s], piece, rx, flip, is_entry)
    order = [(own, j, s) for own in (True, False) for s in range(PARTS) for j in (0, 1)]
    for at, (own, j, s) in enumerate(order):
        own_piece(half if own else 1 - half, j, s, own)
        if at + 2 < 8:
            exchange(at + 2)
        if at >= LAG:
            own, j, s = order[at - LAG]
            side_pieces(half if own else 1 - half, j, s)
    for own, j, s in order[len(order) - LAG:]:
        side_pieces(half if own else 1 - half, j, s)
    for own, j, s in order:
        piece, rx = piece_of(half if own else 1 - half, j, far, s)
        wait_rx(piece, rx)

    slab_done = local(slab, slab_out, cross_loc.at[0])

    holder = half == (z // 2) % 2
    lane = core == z // 4
    owner = holder & lane & (y == x)

    @pl.when(owner)
    def _():
        copies = [local(slab.at[m // 2, m % 2, pl.ds(2 * (z % 2), 2)], col.at[m], loc.at[m]) for m in range(4)]
        for copy in copies:
            copy.wait()

    for step in (2, 1, 3):
        to = (y + step) % 4
        send(col.at[to], col.at[to], col_rx.at[to], at_y(step), owner)
    wait_rx(col.at[y], col_rx.at[y], lane & jnp.logical_not(owner))
    send(col.at[y], col.at[y], col_rx.at[y], flip, holder & lane)
    for step in (2, 1, 3):
        to = (y + step) % 4
        send(col.at[y], col.at[y], col_rx.at[y], at_y(step), lane & jnp.logical_not(holder & (to == x)))
    send(col.at[y], col.at[y], col_rx.at[y], partner, lane)
    for step in (1, 3, 2):
        m = (y + step) % 4
        wait_rx(col.at[m], col_rx.at[m], lane & jnp.logical_not(owner))
        send(col.at[m], col.at[m], col_rx.at[m], partner, lane)
    for m in range(4):
        wait_rx(col.at[m], col_rx.at[m], jnp.logical_not(lane))

    outs = [slab_done, local(col, col_out, loc.at[1])]
    for i in range(8):
        wait_rx(other.at[i], other_rx.at[i])
    outs.append(local(other, other_out, loc.at[2]))
    for copy in outs:
        copy.wait()
    for copy, when in pending:
        if when is None:
            copy.wait_send()
        else:
            pl.when(when)(copy.wait_send)


def move(child_tile):
    f32 = jnp.float32
    any_spec = pl.BlockSpec(memory_space=pl.ANY)
    return pl.pallas_call(
        move_kernel,
        out_shape=(jax.ShapeDtypeStruct((2, 2, 4, 128, 256), f32),
                   jax.ShapeDtypeStruct((4, 2, 128, 256), f32),
                   jax.ShapeDtypeStruct((8, 64, 256), f32)),
        in_specs=[any_spec],
        out_specs=(any_spec, any_spec, any_spec),
        scratch_shapes=[
            pltpu.VMEM((2, 2, 4, 128, 256), f32),
            pltpu.VMEM((4, 2, 128, 256), f32),
            pltpu.VMEM((PARTS, 128 // PARTS, 256), f32),
            pltpu.VMEM((8, 64, 256), f32),
            pltpu.SemaphoreType.DMA((2, 2, 4, PARTS)),
            pltpu.SemaphoreType.DMA((4,)),
            pltpu.SemaphoreType.DMA((PARTS,)),
            pltpu.SemaphoreType.DMA((8,)),
            pltpu.SemaphoreType.DMA((32 + 32 * PARTS,)),
            pltpu.SemaphoreType.DMA((4,)),
            pltpu.SemaphoreType.DMA((PARTS,)),
        ],
        compiler_params=pltpu.CompilerParams(collective_id=0, has_side_effects=True),
    )(child_tile)


def split(value):
    high = value.astype(jnp.bfloat16)
    return high, (value - high.astype(jnp.float32)).astype(jnp.bfloat16)


def dot3(a_high, a_low, b_high, b_low):
    def dot(a, b):
        return lax.dot_general(a, b, (((1,), (1,)), ((), ())), preferred_element_type=jnp.float32)
    return dot(a_high, b_high) + (dot(a_high, b_low) + dot(a_low, b_high))


def weights(maps, k, triple):
    first = maps[k, 2 * triple] - 3 * triple
    second = maps[k, 2 * triple + 1] - 3 * triple
    return [jnp.where(t, 1.0, 0.0).astype(jnp.float32) for t in (first == 0, first == 1, second == 1, second == 2)]


def expand(pairs, row_weights, col_weights):
    total = [[None] * 3 for _ in range(3)]
    for (first, second), rw, cw in zip(pairs, row_weights, col_weights):
        rows = (first * rw[0], first * rw[1] + second * rw[2], second * rw[3])
        for p, value in enumerate(rows):
            left, right = value[:, :BLK], value[:, BLK:]
            for q, part in enumerate((left * cw[0], left * cw[1] + right * cw[2], right * cw[3])):
                total[p][q] = part if total[p][q] is None else total[p][q] + part
    return total


def front_kernel(maps, pattern, inverse_in, child_in, other_in, slab_in, col_in, out,
                 inverse, child, other, slab, col, arrived, inv_high, inv_low, tile_high, tile_low, fac_high, fac_low):
    half = lax.axis_index("half")
    row = lax.axis_index("row")
    colix = lax.axis_index("col")
    slab_index = 2 * row + half
    copies = [pltpu.make_async_copy(src, dst, arrived.at[i]) for i, (src, dst) in enumerate((
        (inverse_in, inverse), (slab_in, slab), (col_in, col),
        (child_in.at[pl.ds(half * 512, 512)], child), (other_in, other)))]
    for copy in copies:
        copy.start()
    copies[0].wait()
    for b in range(6):
        rows = slice(b * BLK, (b + 1) * BLK)
        inv_high[rows], inv_low[rows] = split(inverse[rows])
    copies[1].wait()
    panel_cols = [[weights(maps, k, j) for k in (0, 1)] for j in (0, 1)]
    for t in range(3):
        if t == 2:
            copies[2].wait()
        triple = 2 * slab_index + t if t < 2 else colix
        row_weights = [weights(maps, k, triple) for k in (0, 1)]
        for j in range(2):
            if t < 2:
                pairs = [(slab[k, j, 2 * t], slab[k, j, 2 * t + 1]) for k in (0, 1)]
            else:
                pairs = [(col[2 * k + j, 0], col[2 * k + j, 1]) for k in (0, 1)]
            blocks = expand(pairs, row_weights, panel_cols[j])
            for p in range(3):
                for q in range(3):
                    high, low = split(blocks[p][q])
                    where = (slice(p * BLK, (p + 1) * BLK), slice((3 * j + q) * BLK, (3 * j + q + 1) * BLK))
                    tile_high[t, where[0], where[1]] = high
                    tile_low[t, where[0], where[1]] = low
        for n in range(3):
            depth = (n + 1) * 256
            cols = slice(n * 256, depth)
            product = dot3(tile_high[t, :, :depth], tile_low[t, :, :depth],
                           inv_high[cols, :depth], inv_low[cols, :depth])
            for p in range(3):
                for q in range(2):
                    b = 2 * n + q
                    block = product[p * BLK:(p + 1) * BLK, q * BLK:(q + 1) * BLK]
                    block = block * pattern[3 * triple + p, b].astype(jnp.float32)
                    rows = slice(t * 384 + p * BLK, t * 384 + (p + 1) * BLK)
                    high, low = split(block)
                    fac_high[rows, b * BLK:(b + 1) * BLK] = high
                    fac_low[rows, b * BLK:(b + 1) * BLK] = low
                    if t < 2:
                        @pl.when(colix == b // 3)
                        def _(rows=rows, b=b, block=block):
                            out[rows, (b % 3) * BLK:(b % 3 + 1) * BLK] = block

    copies[3].wait()
    copies[4].wait()

    @pl.when(colix >= 2)
    def _():
        col_weights = [weights(maps, k, colix) for k in (0, 1)]
        keep = slab_index == 0
        for t in range(2):
            schur = dot3(fac_high[t * 384:(t + 1) * 384], fac_low[t * 384:(t + 1) * 384],
                         fac_high[768:], fac_low[768:])
            row_weights = [weights(maps, k, 2 * slab_index + t) for k in (0, 1)]
            own = [child[t * 256 + i * BLK:t * 256 + (i + 1) * BLK, :] for i in (0, 1)]
            sent = [other[4 * t + 2 * i:4 * t + 2 * i + 2].reshape(BLK, 256) for i in (0, 1)]
            ordered = [[jnp.where(half == k, a, b) for a, b in zip(own, sent)] for k in (0, 1)]
            blocks = expand(ordered, row_weights, col_weights)
            for p in range(3):
                for q in range(3):
                    term = schur[p * BLK:(p + 1) * BLK, q * BLK:(q + 1) * BLK]
                    out[t * 384 + p * BLK:t * 384 + (p + 1) * BLK, q * BLK:(q + 1) * BLK] = (
                        blocks[p][q] - jnp.where(keep, 0.0, term))


def local(child_updates, child_maps, panel_pattern, pivot_inverse):
    child_tile = child_updates[0]
    slab, col, other = move(child_tile)
    smem = pl.BlockSpec(memory_space=pltpu.SMEM)
    vmem = pl.BlockSpec(memory_space=pltpu.VMEM)
    bf16, f32 = jnp.bfloat16, jnp.float32
    hbm = pl.BlockSpec(memory_space=pl.ANY)
    result = pl.pallas_call(
        front_kernel,
        out_shape=jax.ShapeDtypeStruct((768, 384), jnp.float32),
        in_specs=[smem, smem] + [hbm] * 5,
        out_specs=vmem,
        scratch_shapes=[
            pltpu.VMEM((768, 768), f32),
            pltpu.VMEM((512, 256), f32),
            pltpu.VMEM((8, 64, 256), f32),
            pltpu.VMEM((2, 2, 4, 128, 256), f32),
            pltpu.VMEM((4, 2, 128, 256), f32),
            pltpu.SemaphoreType.DMA((5,)),
            pltpu.VMEM((768, 768), bf16),
            pltpu.VMEM((768, 768), bf16),
            pltpu.VMEM((3, 384, 768), bf16),
            pltpu.VMEM((3, 384, 768), bf16),
            pltpu.VMEM((1152, 768), bf16),
            pltpu.VMEM((1152, 768), bf16),
        ],
        compiler_params=pltpu.CompilerParams(vmem_limit_bytes=60 * 2**20),
    )(child_maps, panel_pattern, pivot_inverse, child_tile, other, slab, col)
    return result.reshape(1, 1, 768, 384)


def solution(mesh):
    placed = (P("half", "row", "col"), P(), P(), P())
    return jax.shard_map(
        local, mesh=mesh, in_specs=placed, out_specs=P("row", "half", None, "col"), check_vma=False
    )
```
